32 devices in a mesh: gauss: 4 (over y, core), tile: 8 (over z, x).
Axes of the slice: x: 2, y: 2, z: 4, core: 2. Of those that a mesh axis runs over, the one named last changes fastest.
Arguments:
- params: float32 [59, 16384], P(None, ('gauss', 'tile')), as said below
- moment_one: float32 [59, 16384], P(None, ('gauss', 'tile')), may hold values from -1.8 to 1.8
- moment_two: float32 [59, 16384], P(None, ('gauss', 'tile')), may hold values from 1e-06 to 0.01
- camera: float32 [3, 11], replicated, as said below
- target: float32 [3, 3, 32, 256], P(None, None, ('gauss', 'tile')), may hold values from 0 to 1
- tile_ids: int32 [3, 32], P(None, ('gauss', 'tile')), may hold values from 0 to 31, as said below
- splat_lists: int32 [3, 32, 256], P(None, ('gauss', 'tile')), may hold values from 0 to 16383, as said below
- counts: int32 [3, 32], P(None, ('gauss', 'tile')), may hold values from 32 to 256, as said below
Outputs:
- new_params: float32 [59, 16384], P(None, ('gauss', 'tile'))
- new_first: float32 [59, 16384], P(None, ('gauss', 'tile'))
- new_second: float32 [59, 16384], P(None, ('gauss', 'tile'))
- rendered: float32 [3, 3, 32, 256], P(None, None, ('gauss', 'tile'))
- view_losses: float32 [3], replicated
The draws below stay inside these ranges and needn't reach their ends.
Inputs may be any that keep to these rules, and one draw needn't show every extreme that they name: `splat_lists`: entries of slot q lie in [b * 4096, (b + 1) * 4096) with b = q // 8; entries at or past the slot's count are padding. `counts`: every view has a slot whose count is 256. `tile_ids`: in each view the slots q with q // 8 = b hold each tile of b * 8 to (b + 1) * 8 - 1 once. `params`: row 6 lies in [0.5, 1.5]. `camera`: entries 8 to 10 of each row form a unit vector.
All inputs are finite; a program needn't handle non-finite values.
Results may differ from the reference program's by a relative error of at most 0.0003.
Values sent between devices are 32-bit elements; how exact they have to be, the bound alone decides.
A program may use at most 64 MiB of HBM per device.

```python
import math
import jax
import jax.numpy as jnp
from jax import lax

PARAMS = 59
LIST = 256
VIEWS = 3
TILES_WIDE = 4
BAND_G = 4096
BAND_TILES = 8
GAUSS = 16384
TILES = 32


def layout(key):
    base = jax.random.fold_in(key, 11)
    bands = GAUSS // BAND_G
    order = jax.vmap(lambda subkey: jax.random.permutation(subkey, BAND_G))(jax.random.split(jax.random.fold_in(base, 1), bands))
    shuffled = jax.vmap(lambda subkey: jax.random.permutation(subkey, BAND_TILES))(jax.random.split(jax.random.fold_in(base, 2), VIEWS * bands))
    tiles = shuffled.reshape(VIEWS, bands, BAND_TILES) + (jnp.arange(bands) * BAND_TILES)[None, :, None]
    return (order.astype(jnp.int32), tiles.reshape(VIEWS, TILES).astype(jnp.int32))


def draw_params(key, part):
    order, tiles = layout(key)
    bands = GAUSS // BAND_G
    per_home = BAND_G // BAND_TILES
    spread = jnp.broadcast_to(jnp.arange(BAND_G, dtype=jnp.int32)[None, :] // per_home, (bands, BAND_G))
    home = jnp.zeros((bands, BAND_G), jnp.int32).at[jnp.arange(bands)[:, None], order].set(spread)
    home = (home + jnp.arange(bands, dtype=jnp.int32)[:, None] * BAND_TILES).reshape(GAUSS)
    keys = jax.random.split(jax.random.fold_in(key, 21), 8)
    place_x = (home % TILES_WIDE * 16).astype(jnp.float32) + 16.0 * jax.random.uniform(keys[0], (GAUSS,))
    place_y = (home // TILES_WIDE * 16).astype(jnp.float32) + 16.0 * jax.random.uniform(keys[1], (GAUSS,))
    depth = jax.random.uniform(keys[2], (GAUSS,), minval=-1.0, maxval=1.0)
    log_scale = jax.random.uniform(keys[3], (3, GAUSS), minval=-3.8, maxval=-2.4)
    quat_w = jax.random.uniform(keys[4], (1, GAUSS), minval=0.5, maxval=1.5)
    quat_rest = jnp.clip(0.5 * jax.random.normal(keys[5], (3, GAUSS)), -1.5, 1.5)
    logit = jnp.clip(-4.0 + jax.random.normal(keys[6], (1, GAUSS)), -8.0, 0.0)
    coeffs = 0.6 * jax.random.normal(keys[7], (48, GAUSS))
    centres = jnp.stack([place_x / 64.0, place_y / 64.0, depth])
    return jnp.concatenate([centres, log_scale, quat_w, quat_rest, logit, coeffs], axis=0).astype(jnp.float32)


def draw_tile_ids(key, part):
    return layout(key)[1]


def draw_splat_lists(key, part):
    order, tiles = layout(key)
    per_home = BAND_G // BAND_TILES
    rows_band = BAND_TILES // TILES_WIDE
    keys = jax.random.split(jax.random.fold_in(key, 31), 3)
    band = jnp.arange(TILES, dtype=jnp.int32) // BAND_TILES
    local_tile = tiles - band[None, :] * BAND_TILES
    step_row = (jax.random.randint(keys[0], (VIEWS, TILES, LIST), 0, 4) + 1) // 2 - 1
    step_col = (jax.random.randint(keys[1], (VIEWS, TILES, LIST), 0, 4) + 1) // 2 - 1
    near_row = jnp.clip(local_tile[:, :, None] // TILES_WIDE + step_row, 0, rows_band - 1)
    near_col = jnp.clip(local_tile[:, :, None] % TILES_WIDE + step_col, 0, TILES_WIDE - 1)
    chosen = (near_row * TILES_WIDE + near_col) * per_home + jax.random.randint(keys[2], (VIEWS, TILES, LIST), 0, per_home)
    band_full = jnp.broadcast_to(band[None, :, None], (VIEWS, TILES, LIST))
    return (order[band_full, chosen] + band_full * BAND_G).astype(jnp.int32)


def draw_counts(key, part):
    divisor = jax.random.randint(jax.random.fold_in(key, 41), (VIEWS, TILES), 1, 9)
    filled = (LIST // divisor).at[:, 0].set(LIST)
    return filled.astype(jnp.int32)


def draw_camera(key, part):
    keys = jax.random.split(jax.random.fold_in(key, 51), 4)
    jitter = jax.random.uniform(keys[0], (VIEWS, 4), minval=-0.02, maxval=0.02)
    shear = jax.random.uniform(keys[1], (VIEWS, 2), minval=-4.0, maxval=4.0)
    offset = jax.random.uniform(keys[2], (VIEWS, 2), minval=-3.0, maxval=3.0)
    tilt = jax.random.uniform(keys[3], (VIEWS, 2), minval=-0.4, maxval=0.4)
    length = jnp.sqrt(1.0 + tilt[:, 0] * tilt[:, 0] + tilt[:, 1] * tilt[:, 1])
    rows = jnp.stack([64.0 * (1.0 + jitter[:, 0]), 64.0 * jitter[:, 1], shear[:, 0], 64.0 * jitter[:, 2], 64.0 * (1.0 + jitter[:, 3]), shear[:, 1], offset[:, 0], offset[:, 1], tilt[:, 0] / length, tilt[:, 1] / length, 1.0 / length], axis=1)
    return rows.astype(jnp.float32)


def level_of(rng, shape, cuts, low, largest):
    def one(position, shards_of):
        draws = jax.random.uniform(jax.random.fold_in(jax.random.fold_in(rng, 6), position), (shards_of,), jnp.float32, low / len(cuts), largest / len(cuts))
        return jnp.repeat(jnp.exp(draws), shape[position] // shards_of).reshape((-1,) + (1,) * (len(shape) - position - 1))

    gain = one(*cuts[0])
    for cut in cuts[1:]:
        gain = gain * one(*cut)
    return gain


def normal_values(own_key, dims, scale, most, cuts=(), kind=jnp.bfloat16):
    values = jax.random.normal(own_key, dims, jnp.float32) * scale
    if len(cuts) > 0:
        values = level_of(own_key, dims, cuts, -0.22, 0.18) * values
    return jnp.clip(values, min=-most, max=most).astype(kind)


def setup_inputs(seed: int = 0) -> dict:
    streams_of = jax.random.split(jax.random.key(seed), 9)
    return {
        "params": draw_params(jax.random.fold_in(streams_of[8], 71), 0),
        "moment_one": normal_values(streams_of[1], (PARAMS, GAUSS), 0.3, 1.8, ((1, 32),), jnp.float32),
        "moment_two": jnp.clip(jnp.exp(math.log(0.01) - 9.2103404 * jax.random.uniform(streams_of[2], (PARAMS, GAUSS), jnp.float32) ** level_of(streams_of[2], (PARAMS, GAUSS), ((1, 32),), -0.2, 0.2)), 9.999999974752427e-07, 0.01),
        "camera": draw_camera(jax.random.fold_in(streams_of[8], 71), 0),
        "target": jnp.clip(1.0 * jax.random.uniform(streams_of[4], (VIEWS, 3, TILES, 256), jnp.float32) ** level_of(streams_of[4], (VIEWS, 3, TILES, 256), ((2, 32),), -0.2, 0.2), 0.0, 1.0),
        "tile_ids": draw_tile_ids(jax.random.fold_in(streams_of[8], 71), 0),
        "splat_lists": draw_splat_lists(jax.random.fold_in(streams_of[8], 71), 0),
        "counts": draw_counts(jax.random.fold_in(streams_of[8], 71), 0),
    }


band_zero = 0.28209479177387814
band_one = 0.4886025119029199
band_two = (1.0925484305920792, -1.0925484305920792, 0.31539156525252005, -1.0925484305920792, 0.5462742152960396)
band_three = (-0.5900435899266435, 2.890611442640554, -0.4570457994644658, 0.3731763325901154, -0.4570457994644658, 1.445305721320277, -0.5900435899266435)
learning_rates = (0.00016,) * 3 + (0.005,) * 3 + (0.001,) * 4 + (0.05,) + (0.0025,) * 3 + (0.000125,) * 45
highest = lax.Precision.HIGHEST

def harmonics(facing):
    facing_x, facing_y, facing_z = (facing[0], facing[1], facing[2])
    square_x, square_y, square_z = (facing_x * facing_x, facing_y * facing_y, facing_z * facing_z)
    return jnp.stack([band_zero + 0.0 * facing_x, -band_one * facing_y, band_one * facing_z, -band_one * facing_x, band_two[0] * facing_x * facing_y, band_two[1] * facing_y * facing_z, band_two[2] * (2.0 * square_z - square_x - square_y), band_two[3] * facing_x * facing_z, band_two[4] * (square_x - square_y), band_three[0] * facing_y * (3.0 * square_x - square_y), band_three[1] * facing_x * facing_y * facing_z, band_three[2] * facing_y * (4.0 * square_z - square_x - square_y), band_three[3] * facing_z * (2.0 * square_z - 3.0 * square_x - 3.0 * square_y), band_three[4] * facing_x * (4.0 * square_z - square_x - square_y), band_three[5] * facing_z * (square_x - square_y), band_three[6] * facing_x * (square_x - 3.0 * square_y)])

def project(params, camera):
    quaternion = params[6:10]
    quat_norm = jnp.sqrt(lax.optimization_barrier(jnp.sum(quaternion * quaternion, axis=0)))
    quat_w, quat_x, quat_y, quat_z = [quaternion[component] / quat_norm for component in range(4)]
    rotation = jnp.stack([1.0 - 2.0 * (quat_y * quat_y + quat_z * quat_z), 2.0 * (quat_x * quat_y - quat_w * quat_z), 2.0 * (quat_x * quat_z + quat_w * quat_y), 2.0 * (quat_x * quat_y + quat_w * quat_z), 1.0 - 2.0 * (quat_x * quat_x + quat_z * quat_z), 2.0 * (quat_y * quat_z - quat_w * quat_x), 2.0 * (quat_x * quat_z - quat_w * quat_y), 2.0 * (quat_y * quat_z + quat_w * quat_x), 1.0 - 2.0 * (quat_x * quat_x + quat_y * quat_y)]).reshape(3, 3, -1)
    stretched = rotation * jnp.exp(params[3:6])[None, :, :]
    affine = camera[0:6].reshape(2, 3)
    screen_axes = jnp.einsum('ki,ijn->kjn', affine, stretched, precision=highest)
    cov_a = lax.optimization_barrier(jnp.sum(screen_axes[0] * screen_axes[0], axis=0)) + 0.3
    cov_b = lax.optimization_barrier(jnp.sum(screen_axes[0] * screen_axes[1], axis=0))
    cov_c = lax.optimization_barrier(jnp.sum(screen_axes[1] * screen_axes[1], axis=0)) + 0.3
    determinant = cov_a * cov_c - cov_b * cov_b
    centre_px = jnp.einsum('ki,in->kn', affine, params[0:3], precision=highest) + camera[6:8][:, None]
    opacity = jax.nn.sigmoid(params[10])
    coeffs = params[11:59].reshape(16, 3, -1)
    colour = jnp.maximum(jnp.einsum('i,ikn->kn', harmonics(camera[8:11]), coeffs, precision=highest) + 0.5, 0.0)
    return jnp.concatenate([centre_px, jnp.stack([cov_c / determinant, -cov_b / determinant, cov_a / determinant, opacity]), colour], axis=0)

def shade(splat_attrs, live_count, tile_id):
    pixel_index = jnp.arange(256, dtype=jnp.int32)
    pixel_x = (tile_id % TILES_WIDE * 16 + pixel_index % 16).astype(jnp.float32) + 0.5
    pixel_y = (tile_id // TILES_WIDE * 16 + pixel_index // 16).astype(jnp.float32) + 0.5
    offset_x = pixel_x[:, None] - splat_attrs[0][None, :]
    offset_y = pixel_y[:, None] - splat_attrs[1][None, :]
    exponent = -0.5 * (splat_attrs[2] * offset_x * offset_x + splat_attrs[4] * offset_y * offset_y) - splat_attrs[3] * offset_x * offset_y
    live_slots = jnp.arange(splat_attrs.shape[1], dtype=jnp.int32) < live_count
    coverage = jnp.where(live_slots[None, :], jnp.minimum(0.99, splat_attrs[5] * jnp.exp(exponent)), 0.0)
    log_keep = jnp.log(1.0 - coverage)
    before = jnp.concatenate([jnp.zeros_like(log_keep[:, :1]), jnp.cumsum(log_keep[:, :-1], axis=1)], axis=1)
    weights = coverage * jnp.exp(before)
    return jnp.einsum('pj,kj->kp', weights, splat_attrs[6:9], precision=highest)

def adam(params, moment_one, moment_two, gradient):
    rates = jnp.array(learning_rates, dtype=jnp.float32)[:, None]
    first = 0.9 * moment_one + 0.1 * gradient
    second = 0.999 * moment_two + 0.001 * gradient * gradient
    return (params - rates * first / (jnp.sqrt(second) + 1e-15), first, second)

def reference(params, moment_one, moment_two, camera, target, tile_ids, splat_lists, counts):
    grad_scale = 1.0 / (VIEWS * 256)
    gradient = jnp.zeros_like(params)
    images_all = []
    losses = []
    for view_index in range(VIEWS):
        attrs_all, pullback = jax.vjp(lambda values: project(values, camera[view_index]), params)

        def one_tile(item):
            splat_ids, live_count, tile_id, target_tile = item
            splat_attrs = jnp.take(attrs_all, splat_ids, axis=1)
            colours, tile_back = jax.vjp(lambda values: shade(values, live_count, tile_id), splat_attrs)
            residual = colours - target_tile
            attr_grad, = tile_back(residual * grad_scale)
            return (colours, jnp.sum(residual * residual), attr_grad)
        colours, squared, attr_grads = lax.map(one_tile, (splat_lists[view_index], counts[view_index], tile_ids[view_index], jnp.transpose(target[view_index], (1, 0, 2))))
        flat_grad = jnp.transpose(attr_grads, (1, 0, 2)).reshape(9, -1)
        summed = jnp.zeros_like(attrs_all).at[:, splat_lists[view_index].reshape(-1)].add(flat_grad)
        gradient = gradient + pullback(summed)[0]
        images_all.append(jnp.transpose(colours, (1, 0, 2)))
        losses.append(0.5 * jnp.sum(squared) / (3 * 256 * TILES))
    return adam(params, moment_one, moment_two, gradient) + (jnp.stack(images_all), jnp.stack(losses))
```

```python
import functools

import jax
import jax.numpy as jnp
from jax import lax
from jax.experimental import pallas as pl
from jax.experimental.pallas import tpu as pltpu
from jax.sharding import PartitionSpec as P

MESH = pl.DeviceIdType.MESH
VIEWS = 3
TILES_WIDE = 4


band_zero = 0.28209479177387814
band_one = 0.4886025119029199
band_two = (
    1.0925484305920792,
    -1.0925484305920792,
    0.31539156525252005,
    -1.0925484305920792,
    0.5462742152960396,
)
band_three = (
    -0.5900435899266435,
    2.890611442640554,
    -0.4570457994644658,
    0.3731763325901154,
    -0.4570457994644658,
    1.445305721320277,
    -0.5900435899266435,
)
learning_rates = (
    (0.00016,) * 3 + (0.005,) * 3 + (0.001,) * 4 + (0.05,) + (0.0025,) * 3 + (0.000125,) * 45
)
highest = lax.Precision.HIGHEST


def split(value, parts):
    pieces = []
    rest = value
    for _ in range(parts - 1):
        piece = rest.astype(jnp.bfloat16)
        pieces.append(piece)
        rest = rest - piece.astype(jnp.float32)
    pieces.append(rest.astype(jnp.bfloat16))
    return pieces


def dot(left, right, dims, precision=None):
    return lax.dot_general(
        left, right, (dims, ((), ())), precision=precision, preferred_element_type=jnp.float32
    )


def harmonics(x, y, z):
    xx, yy, zz = x * x, y * y, z * z
    return [
        band_zero + 0.0 * x,
        -band_one * y,
        band_one * z,
        -band_one * x,
        band_two[0] * x * y,
        band_two[1] * y * z,
        band_two[2] * (2.0 * zz - xx - yy),
        band_two[3] * x * z,
        band_two[4] * (xx - yy),
        band_three[0] * y * (3.0 * xx - yy),
        band_three[1] * x * y * z,
        band_three[2] * y * (4.0 * zz - xx - yy),
        band_three[3] * z * (2.0 * zz - 3.0 * xx - 3.0 * yy),
        band_three[4] * x * (4.0 * zz - xx - yy),
        band_three[5] * z * (xx - yy),
        band_three[6] * x * (xx - 3.0 * yy),
    ]


def iota(shape, dim):
    return lax.broadcasted_iota(jnp.int32, shape, dim)


def basis(camera, n_params):
    rows = 8 * VIEWS
    row, lane = iota((rows, n_params), 0), iota((rows, n_params), 1)
    quantity, view = row % 8, row // 8

    def entry(index):
        value = jnp.full((rows, n_params), camera[VIEWS - 1, index], jnp.float32)
        for v in range(VIEWS - 1):
            value = jnp.where(view == v, camera[v, index], value)
        return value

    out = jnp.zeros((rows, n_params), jnp.float32)
    for k in range(2):
        for i in range(3):
            out = jnp.where((quantity == k) & (lane == i), entry(3 * k + i), out)
    term, channel = (lane - 11) // 3, (lane - 11) % 3
    own = (lane >= 11) & (channel == quantity - 5)
    for i, value in enumerate(harmonics(entry(8), entry(9), entry(10))):
        out = jnp.where(own & (term == i), value, out)
    return out


def kernel(
    n_tile,
    n_gauss,
    params_ref,
    camera,
    target_ref,
    tile_ids,
    lists_ref,
    counts,
    grad_ref,
    image_ref,
    loss_ref,
    attrs,
    parts,
    totals,
    upper,
    lower,
    alpha_ref,
    raw_ref,
    log_ref,
    send_a,
    recv_a,
    send_g,
    recv_g,
    send_l,
    recv_l,
):
    me, mg = lax.axis_index("tile"), lax.axis_index("gauss")
    n_params, own = params_ref.shape
    blocks = own // 128
    size = lists_ref.shape[2]
    rows = 8 * VIEWS
    id_row = blocks * rows + 8
    scale = 1.0 / (VIEWS * 256)

    barrier = pltpu.get_barrier_semaphore()
    for d in range(1, n_tile):
        pl.semaphore_signal(
            barrier, inc=1, device_id={"tile": lax.rem(me + d, n_tile)}, device_id_type=MESH
        )
    for d in range(1, n_gauss):
        pl.semaphore_signal(
            barrier, inc=1, device_id={"gauss": lax.rem(mg + d, n_gauss)}, device_id_type=MESH
        )

    table = basis(camera, n_params)
    view_of = iota((VIEWS, own), 0)

    def entry(index):
        value = jnp.full((VIEWS, own), camera[VIEWS - 1, index], jnp.float32)
        for v in range(VIEWS - 1):
            value = jnp.where(view_of == v, camera[v, index], value)
        return value

    affine = [[entry(3 * k + i) for i in range(3)] for k in range(2)]
    params = params_ref[...]
    quat = [params_ref[6 + i : 7 + i, :] for i in range(4)]
    norm = jnp.sqrt(quat[0] * quat[0] + quat[1] * quat[1] + quat[2] * quat[2] + quat[3] * quat[3])
    w, x, y, z = [part / norm for part in quat]
    rot = [
        [1.0 - 2.0 * (y * y + z * z), 2.0 * (x * y - w * z), 2.0 * (x * z + w * y)],
        [2.0 * (x * y + w * z), 1.0 - 2.0 * (x * x + z * z), 2.0 * (y * z - w * x)],
        [2.0 * (x * z - w * y), 2.0 * (y * z + w * x), 1.0 - 2.0 * (x * x + y * y)],
    ]
    stretch = [jnp.exp(params_ref[3 + j : 4 + j, :]) for j in range(3)]
    axes = [
        [sum(affine[k][i] * (rot[i][j] * stretch[j]) for i in range(3)) for j in range(3)]
        for k in range(2)
    ]
    cov_a = sum(axes[0][j] * axes[0][j] for j in range(3)) + 0.3
    cov_b = sum(axes[0][j] * axes[1][j] for j in range(3))
    cov_c = sum(axes[1][j] * axes[1][j] for j in range(3)) + 0.3
    determinant = cov_a * cov_c - cov_b * cov_b
    conic = [cov_c / determinant, -cov_b / determinant, cov_a / determinant]
    opacity = jax.nn.sigmoid(params_ref[10:11, :])

    linear = dot(table, params, ((1,), (0,)), highest)
    quantity = iota((8, own), 0)
    linear_views = []
    for v in range(VIEWS):
        shift = jnp.where(
            quantity == 0, camera[v, 6], jnp.where(quantity == 1, camera[v, 7], 0.5)
        )
        value = linear[8 * v : 8 * v + 8] + shift
        linear_views.append(value)
        value = jnp.where(quantity >= 5, jnp.maximum(value, 0.0), value)
        for q in range(3):
            value = jnp.where(quantity == 2 + q, conic[q][v : v + 1], value)
        for b in range(blocks):
            attrs[me, b * rows + 8 * v : b * rows + 8 * v + 8, :] = value[
                :, 128 * b : 128 * b + 128
            ]
    base = mg * (own * n_tile)
    spare = attrs.shape[1] - blocks * rows
    attrs[me, blocks * rows :, :] = jnp.zeros((spare, 128), jnp.float32)
    for b in range(blocks):
        attrs[me, blocks * rows + b : blocks * rows + b + 1, :] = opacity[
            :, 128 * b : 128 * b + 128
        ]
    for v in range(VIEWS):
        ids = (lists_ref[v] - base).astype(jnp.float32)
        for h in range(size // 128):
            place = id_row + v * (size // 128) + h
            attrs[me, place : place + 1, :] = ids[:, 128 * h : 128 * h + 128]

    pl.semaphore_wait(barrier, n_tile + n_gauss - 2)
    sends = []
    for d in range(1, n_tile):
        copy = pltpu.make_async_remote_copy(
            src_ref=attrs.at[me],
            dst_ref=attrs.at[me],
            send_sem=send_a.at[d],
            recv_sem=recv_a.at[d],
            device_id={"tile": lax.rem(me + d, n_tile)},
            device_id_type=MESH,
        )
        copy.start()
        sends.append(copy)

    before_j = (iota((size, size), 0) < iota((size, size), 1)).astype(jnp.float32)
    after_j = (iota((size, size), 0) > iota((size, size), 1)).astype(jnp.float32)
    for c in range(2):
        upper[c * size : (c + 1) * size, :] = before_j.astype(jnp.bfloat16)
        lower[c * size : (c + 1) * size, :] = after_j.astype(jnp.bfloat16)
    parts[me, rows + 2 * VIEWS : rows + 8, :] = jnp.zeros((8 - 2 * VIEWS, size), jnp.float32)
    for copy in sends:
        copy.wait()

    grad_sends = []
    pixel_col = iota((16, size), 0).astype(jnp.float32) + 0.5
    lane = iota((1, size), 1)
    low_of = iota((128, size), 0)
    op_row = iota((8 * n_tile, size), 0)
    op_high = jnp.where(op_row % 8 < blocks, op_row // 8 * blocks + op_row % 8, -1)
    for v in range(VIEWS):
        ids = lists_ref[v] - base
        high, low = ids // 128, ids % 128
        onehot = (low_of == low).astype(jnp.float32).astype(jnp.bfloat16)
        tiles = [
            attrs[s, b * rows + 8 * v : b * rows + 8 * v + 8, :]
            for s in range(n_tile)
            for b in range(blocks)
        ] + [attrs[s, blocks * rows : blocks * rows + 8, :] for s in range(n_tile)]
        pieces = jnp.concatenate(split(jnp.concatenate(tiles, axis=0), 3), axis=1)
        picked = dot(pieces, jnp.concatenate([onehot] * 3, axis=0), ((1,), (0,)))
        splat = jnp.zeros((8, size), jnp.float32)
        for h in range(n_tile * blocks):
            splat = jnp.where(high == h, picked[8 * h : 8 * h + 8], splat)
        opac = jnp.sum(
            jnp.where(op_high == high, picked[8 * n_tile * blocks :], 0.0), axis=0, keepdims=True
        )
        mean_x, mean_y = splat[0:1], splat[1:2]
        con0, con1, con2 = splat[2:3], splat[3:4], splat[4:5]
        tile = tile_ids[v]
        corner_x = (tile % TILES_WIDE * 16).astype(jnp.float32)
        corner_y = (tile // TILES_WIDE * 16).astype(jnp.float32)
        live = lane < counts[v]
        dx = pixel_col + corner_x - mean_x
        part_x = -0.5 * con0 * dx * dx
        opac_live = jnp.where(live, opac, 0.0)
        dys = []
        for r in range(16):
            dy = (corner_y + (r + 0.5)) - mean_y
            dys.append(dy)
            exponent = part_x - 0.5 * con2 * dy * dy - (con1 * dy) * dx
            raw = jnp.where(live, opac_live * jnp.exp(exponent), 0.0)
            cover = jnp.minimum(0.99, raw)
            log_keep = jnp.log(1.0 - cover)
            alpha_ref[16 * r : 16 * r + 16, :] = cover
            raw_ref[16 * r : 16 * r + 16, :] = jnp.where(
                raw < 0.99, raw, jnp.where(raw == 0.99, 0.5 * raw, 0.0)
            )
            for c, piece in enumerate(split(log_keep, 2)):
                log_ref[16 * r : 16 * r + 16, c * size : (c + 1) * size] = piece
        trans = jnp.exp(dot(log_ref[...], upper[...], ((1,), (0,))))
        cover = alpha_ref[...]
        weights = cover * trans
        w_split = split(weights, 2)
        colour = jnp.where(iota((8, size), 0) < 3, jnp.concatenate([splat[5:8], splat[0:5]], axis=0), 0.0)
        c_split = jnp.concatenate([p.astype(jnp.float32) for p in split(colour, 3)], axis=0)
        c_split = jnp.concatenate([c_split, jnp.zeros_like(colour)], axis=0).astype(jnp.bfloat16)
        image = dot(c_split, w_split[0], ((1,), (1,))) + dot(c_split, w_split[1], ((1,), (1,)))
        image = image[0:8] + image[8:16] + image[16:24]
        residuals = []
        square = jnp.zeros((1, 256), jnp.float32)
        for k in range(3):
            image_ref[v, k] = image[k : k + 1]
            residual = image[k : k + 1] - target_ref[v, k]
            square = square + residual * residual
            residuals.append(residual * scale)
        resid = jnp.concatenate(residuals + [jnp.zeros((5, 256), jnp.float32)], axis=0)
        slope = dot(resid, colour, ((0,), (0,)), highest)
        later = dot(
            jnp.concatenate(split(weights * slope, 2), axis=1), lower[...], ((1,), (0,))
        )
        moved = (trans * slope - later / (1.0 - cover)) * raw_ref[...]
        r_split = jnp.concatenate([p.astype(jnp.float32) for p in split(resid, 3)], axis=0)
        r_split = jnp.concatenate([r_split, jnp.zeros_like(resid)], axis=0).astype(jnp.bfloat16)
        d_colour = dot(r_split, w_split[0], ((1,), (0,))) + dot(r_split, w_split[1], ((1,), (0,)))
        d_colour = d_colour[0:8] + d_colour[8:16] + d_colour[16:24]
        sum0 = jnp.zeros((16, size), jnp.float32)
        sum1 = jnp.zeros((16, size), jnp.float32)
        sum2 = jnp.zeros((16, size), jnp.float32)
        for r in range(16):
            chunk = moved[16 * r : 16 * r + 16]
            first = chunk * dys[r]
            sum0 = sum0 + chunk
            sum1 = sum1 + first
            sum2 = sum2 + first * dys[r]
        m_0 = jnp.sum(sum0, axis=0, keepdims=True)
        m_x = jnp.sum(sum0 * dx, axis=0, keepdims=True)
        m_xx = jnp.sum(sum0 * dx * dx, axis=0, keepdims=True)
        m_y = jnp.sum(sum1, axis=0, keepdims=True)
        m_xy = jnp.sum(sum1 * dx, axis=0, keepdims=True)
        m_yy = jnp.sum(sum2, axis=0, keepdims=True)
        parts[me, 8 * v : 8 * v + 8, :] = jnp.concatenate(
            [
                con0 * m_x + con1 * m_y,
                con1 * m_x + con2 * m_y,
                -0.5 * m_xx,
                -m_xy,
                -0.5 * m_yy,
                d_colour[0:3],
            ],
            axis=0,
        )
        parts[me, rows + v : rows + v + 1, :] = m_0
        parts[me, rows + VIEWS + v : rows + VIEWS + v + 1, :] = square
        start, stop = 8 * v, (8 * v + 8 if v < VIEWS - 1 else rows + 8)
        for d in range(1, n_tile):
            copy = pltpu.make_async_remote_copy(
                src_ref=parts.at[me, start:stop],
                dst_ref=parts.at[me, start:stop],
                send_sem=send_g.at[v, d],
                recv_sem=recv_g.at[v, d],
                device_id={"tile": lax.rem(me + d, n_tile)},
                device_id_type=MESH,
            )
            copy.start()
            grad_sends.append(copy)

    for copy in grad_sends:
        copy.wait()
    squares = sum(parts[s, rows : rows + 8, :] for s in range(n_tile))
    totals[mg] = squares
    loss_sends = []
    for d in range(1, n_gauss):
        copy = pltpu.make_async_remote_copy(
            src_ref=totals.at[mg],
            dst_ref=totals.at[mg],
            send_sem=send_l.at[d],
            recv_sem=recv_l.at[d],
            device_id={"gauss": lax.rem(mg + d, n_gauss)},
            device_id_type=MESH,
        )
        copy.start()
        loss_sends.append(copy)

    op_block = iota((8, size), 0)
    d_views = []
    d_opacity = jnp.zeros((8, 128), jnp.float32)
    for v in range(VIEWS):
        total = jnp.zeros((8 * blocks + 8, 128), jnp.float32)
        for s in range(n_tile):
            place = id_row + v * (size // 128)
            ids = jnp.concatenate(
                [attrs[s, place + h : place + h + 1, :] for h in range(size // 128)], axis=1
            ).astype(jnp.int32)
            block, low = ids // 128 - me * blocks, ids % 128
            onehot = (low_of == low).astype(jnp.float32).astype(jnp.bfloat16)
            part = parts[s, 8 * v : 8 * v + 8, :]
            op_part = parts[s, rows + v : rows + v + 1, :]
            spread = jnp.concatenate(
                [jnp.where(block == b, part, 0.0) for b in range(blocks)]
                + [jnp.where((block == op_block) & (op_block < blocks), op_part, 0.0)],
                axis=0,
            )
            rough = spread.astype(jnp.bfloat16).astype(jnp.float32)
            both = jnp.concatenate([rough, spread - rough], axis=0).astype(jnp.bfloat16)
            added = dot(both, onehot, ((1,), (1,)))
            total = total + added[: 8 * blocks + 8] + added[8 * blocks + 8 :]
        d_views.append(
            jnp.concatenate([total[8 * b : 8 * b + 8] for b in range(blocks)], axis=1)
        )
        d_opacity = d_opacity + total[8 * blocks :]

    d_linear = []
    for v in range(VIEWS):
        value = linear_views[v]
        gate = jnp.where(value > 0.0, 1.0, jnp.where(value == 0.0, 0.5, 0.0))
        d_linear.append(jnp.where(quantity >= 5, gate * d_views[v], d_views[v]))
    grad_ref[...] = dot(table, jnp.concatenate(d_linear, axis=0), ((0,), (0,)), highest)
    g0, g1, g2 = [
        jnp.concatenate([d_views[v][2 + q : 3 + q] for v in range(VIEWS)], axis=0) for q in range(3)
    ]
    q0, q1, q2 = conic
    d_a = -(g0 * q0 * q0 + g1 * q0 * q1 + g2 * q1 * q1)
    d_b = -(2.0 * g0 * q0 * q1 + g1 * (q0 * q2 + q1 * q1) + 2.0 * g2 * q1 * q2)
    d_c = -(g0 * q1 * q1 + g1 * q1 * q2 + g2 * q2 * q2)
    d_axes = [
        [2.0 * d_a * axes[0][j] + d_b * axes[1][j] for j in range(3)],
        [2.0 * d_c * axes[1][j] + d_b * axes[0][j] for j in range(3)],
    ]
    d_mat = [
        [
            jnp.sum(
                affine[0][i] * d_axes[0][j] + affine[1][i] * d_axes[1][j], axis=0, keepdims=True
            )
            for j in range(3)
        ]
        for i in range(3)
    ]
    for j in range(3):
        grad_ref[3 + j : 4 + j, :] = stretch[j] * sum(d_mat[i][j] * rot[i][j] for i in range(3))
    d_rot = [[d_mat[i][j] * stretch[j] for j in range(3)] for i in range(3)]
    sym01, sym02, sym12 = (
        d_rot[0][1] + d_rot[1][0],
        d_rot[0][2] + d_rot[2][0],
        d_rot[1][2] + d_rot[2][1],
    )
    skew01, skew02, skew12 = (
        d_rot[1][0] - d_rot[0][1],
        d_rot[0][2] - d_rot[2][0],
        d_rot[2][1] - d_rot[1][2],
    )
    d_quat = [
        2.0 * (z * skew01 + y * skew02 + x * skew12),
        2.0 * (y * sym01 + z * sym02 - 2.0 * x * (d_rot[1][1] + d_rot[2][2]) + w * skew12),
        2.0 * (x * sym01 + z * sym12 - 2.0 * y * (d_rot[0][0] + d_rot[2][2]) + w * skew02),
        2.0 * (x * sym02 + y * sym12 - 2.0 * z * (d_rot[0][0] + d_rot[1][1]) + w * skew01),
    ]
    along = w * d_quat[0] + x * d_quat[1] + y * d_quat[2] + z * d_quat[3]
    for i, part in enumerate((w, x, y, z)):
        grad_ref[6 + i : 7 + i, :] = (d_quat[i] - part * along) / norm
    d_op = jnp.concatenate([d_opacity[b : b + 1] for b in range(blocks)], axis=1)
    grad_ref[10:11, :] = d_op * (1.0 - opacity)

    for copy in loss_sends:
        copy.wait()
    all_squares = sum(totals[g] for g in range(n_gauss))
    factor = 0.5 / (3 * 256 * n_tile * n_gauss)
    for v in range(VIEWS):
        loss_ref[v] = jnp.sum(all_squares[VIEWS + v : VIEWS + v + 1]) * factor


def shards(params, moment_one, moment_two, camera, target, tile_ids, splat_lists, counts):
    n_tile, n_gauss = lax.axis_size("tile"), lax.axis_size("gauss")
    own = params.shape[1]
    size = splat_lists.shape[2]
    blocks = own // 128
    rows = 8 * VIEWS
    id_rows = -(-(VIEWS * (size // 128)) // 8) * 8
    vmem = pl.BlockSpec(memory_space=pltpu.VMEM)
    smem = pl.BlockSpec(memory_space=pltpu.SMEM)
    dma = pltpu.SemaphoreType.DMA
    gradient, images, losses = pl.pallas_call(
        functools.partial(kernel, n_tile, n_gauss),
        out_shape=(
            jax.ShapeDtypeStruct(params.shape, jnp.float32),
            jax.ShapeDtypeStruct(target.shape, jnp.float32),
            jax.ShapeDtypeStruct((VIEWS,), jnp.float32),
        ),
        in_specs=[vmem, smem, vmem, smem, vmem, smem],
        out_specs=(vmem, vmem, smem),
        scratch_shapes=[
            pltpu.VMEM((n_tile, blocks * rows + 8 + id_rows, 128), jnp.float32),
            pltpu.VMEM((n_tile, rows + 8, size), jnp.float32),
            pltpu.VMEM((n_gauss, 8, size), jnp.float32),
            pltpu.VMEM((2 * size, size), jnp.bfloat16),
            pltpu.VMEM((2 * size, size), jnp.bfloat16),
            pltpu.VMEM((256, size), jnp.float32),
            pltpu.VMEM((256, size), jnp.float32),
            pltpu.VMEM((256, 2 * size), jnp.bfloat16),
            dma((n_tile,)),
            dma((n_tile,)),
            dma((VIEWS, n_tile)),
            dma((VIEWS, n_tile)),
            dma((n_gauss,)),
            dma((n_gauss,)),
        ],
        compiler_params=pltpu.CompilerParams(collective_id=0, has_side_effects=True),
    )(
        params,
        camera,
        target,
        tile_ids.reshape(VIEWS),
        splat_lists,
        counts.reshape(VIEWS),
    )
    rates = jnp.array(learning_rates, dtype=jnp.float32)[:, None]
    first = 0.9 * moment_one + 0.1 * gradient
    second = 0.999 * moment_two + 0.001 * gradient * gradient
    updated = params - rates * first / (jnp.sqrt(second) + 1e-15)
    return (updated, first, second, images, losses)


def solution(mesh):
    return jax.shard_map(
        shards,
        mesh=mesh,
        in_specs=(
            P(None, ("gauss", "tile")),
            P(None, ("gauss", "tile")),
            P(None, ("gauss", "tile")),
            P(),
            P(None, None, ("gauss", "tile"), None),
            P(None, ("gauss", "tile")),
            P(None, ("gauss", "tile"), None),
            P(None, ("gauss", "tile")),
        ),
        out_specs=(
            P(None, ("gauss", "tile")),
            P(None, ("gauss", "tile")),
            P(None, ("gauss", "tile")),
            P(None, None, ("gauss", "tile"), None),
            P(),
        ),
        check_vma=False,
    )
```

```python
import functools

import jax
import jax.numpy as jnp
from jax import lax
from jax.experimental import pallas as pl
from jax.experimental.pallas import tpu as pltpu
from jax.sharding import PartitionSpec as P

MESH = pl.DeviceIdType.MESH
VIEWS = 3
TILES_WIDE = 4


band_zero = 0.28209479177387814
band_one = 0.4886025119029199
band_two = (
    1.0925484305920792,
    -1.0925484305920792,
    0.31539156525252005,
    -1.0925484305920792,
    0.5462742152960396,
)
band_three = (
    -0.5900435899266435,
    2.890611442640554,
    -0.4570457994644658,
    0.3731763325901154,
    -0.4570457994644658,
    1.445305721320277,
    -0.5900435899266435,
)
learning_rates = (
    (0.00016,) * 3 + (0.005,) * 3 + (0.001,) * 4 + (0.05,) + (0.0025,) * 3 + (0.000125,) * 45
)
highest = lax.Precision.HIGHEST


def split(value, parts):
    pieces = []
    rest = value
    for _ in range(parts - 1):
        piece = rest.astype(jnp.bfloat16)
        pieces.append(piece)
        rest = rest - piece.astype(jnp.float32)
    pieces.append(rest.astype(jnp.bfloat16))
    return pieces


def dot(left, right, dims, precision=None):
    return lax.dot_general(
        left, right, (dims, ((), ())), precision=precision, preferred_element_type=jnp.float32
    )


def harmonics(x, y, z):
    xx, yy, zz = x * x, y * y, z * z
    return [
        band_zero + 0.0 * x,
        -band_one * y,
        band_one * z,
        -band_one * x,
        band_two[0] * x * y,
        band_two[1] * y * z,
        band_two[2] * (2.0 * zz - xx - yy),
        band_two[3] * x * z,
        band_two[4] * (xx - yy),
        band_three[0] * y * (3.0 * xx - yy),
        band_three[1] * x * y * z,
        band_three[2] * y * (4.0 * zz - xx - yy),
        band_three[3] * z * (2.0 * zz - 3.0 * xx - 3.0 * yy),
        band_three[4] * x * (4.0 * zz - xx - yy),
        band_three[5] * z * (xx - yy),
        band_three[6] * x * (xx - 3.0 * yy),
    ]


def iota(shape, dim):
    return lax.broadcasted_iota(jnp.int32, shape, dim)


def basis(camera, n_params):
    rows = 8 * VIEWS
    row, lane = iota((rows, n_params), 0), iota((rows, n_params), 1)
    quantity, view = row % 8, row // 8

    def entry(index):
        value = jnp.full((rows, n_params), camera[VIEWS - 1, index], jnp.float32)
        for v in range(VIEWS - 1):
            value = jnp.where(view == v, camera[v, index], value)
        return value

    out = jnp.zeros((rows, n_params), jnp.float32)
    for k in range(2):
        for i in range(3):
            out = jnp.where((quantity == k) & (lane == i), entry(3 * k + i), out)
    term, channel = (lane - 11) // 3, (lane - 11) % 3
    own = (lane >= 11) & (channel == quantity - 5)
    for i, value in enumerate(harmonics(entry(8), entry(9), entry(10))):
        out = jnp.where(own & (term == i), value, out)
    return out


def kernel(
    n_tile,
    n_gauss,
    params_ref,
    camera,
    target_ref,
    tile_ids,
    lists_ref,
    counts,
    grad_ref,
    image_ref,
    loss_ref,
    attrs,
    parts,
    totals,
    upper,
    lower,
    alpha_ref,
    raw_ref,
    log_ref,
    send_a,
    recv_a,
    send_g,
    recv_g,
    send_l,
    recv_l,
):
    me, mg = lax.axis_index("tile"), lax.axis_index("gauss")
    n_params, own = params_ref.shape
    blocks = own // 128
    size = lists_ref.shape[2]
    rows = 8 * VIEWS
    view_rows = 8 * blocks
    id_row = 8 + VIEWS * view_rows
    scale = 1.0 / (VIEWS * 256)

    barrier = pltpu.get_barrier_semaphore()
    for d in range(1, n_tile):
        pl.semaphore_signal(
            barrier, inc=1, device_id={"tile": lax.rem(me + d, n_tile)}, device_id_type=MESH
        )
    for d in range(1, n_gauss):
        pl.semaphore_signal(
            barrier, inc=1, device_id={"gauss": lax.rem(mg + d, n_gauss)}, device_id_type=MESH
        )

    table = basis(camera, n_params)
    view_of = iota((VIEWS, own), 0)

    def entry(index):
        value = jnp.full((VIEWS, own), camera[VIEWS - 1, index], jnp.float32)
        for v in range(VIEWS - 1):
            value = jnp.where(view_of == v, camera[v, index], value)
        return value

    affine = [[entry(3 * k + i) for i in range(3)] for k in range(2)]
    params = params_ref[...]
    quat = [params_ref[6 + i : 7 + i, :] for i in range(4)]
    norm = jnp.sqrt(quat[0] * quat[0] + quat[1] * quat[1] + quat[2] * quat[2] + quat[3] * quat[3])
    w, x, y, z = [part / norm for part in quat]
    rot = [
        [1.0 - 2.0 * (y * y + z * z), 2.0 * (x * y - w * z), 2.0 * (x * z + w * y)],
        [2.0 * (x * y + w * z), 1.0 - 2.0 * (x * x + z * z), 2.0 * (y * z - w * x)],
        [2.0 * (x * z - w * y), 2.0 * (y * z + w * x), 1.0 - 2.0 * (x * x + y * y)],
    ]
    stretch = [jnp.exp(params_ref[3 + j : 4 + j, :]) for j in range(3)]
    axes = [
        [sum(affine[k][i] * (rot[i][j] * stretch[j]) for i in range(3)) for j in range(3)]
        for k in range(2)
    ]
    cov_a = sum(axes[0][j] * axes[0][j] for j in range(3)) + 0.3
    cov_b = sum(axes[0][j] * axes[1][j] for j in range(3))
    cov_c = sum(axes[1][j] * axes[1][j] for j in range(3)) + 0.3
    determinant = cov_a * cov_c - cov_b * cov_b
    conic = [cov_c / determinant, -cov_b / determinant, cov_a / determinant]
    opacity = jax.nn.sigmoid(params_ref[10:11, :])

    linear = dot(table, params, ((1,), (0,)), highest)
    quantity = iota((8, own), 0)
    linear_views = []
    for v in range(VIEWS):
        shift = jnp.where(
            quantity == 0, camera[v, 6], jnp.where(quantity == 1, camera[v, 7], 0.5)
        )
        value = linear[8 * v : 8 * v + 8] + shift
        linear_views.append(value)
        value = jnp.where(quantity >= 5, jnp.maximum(value, 0.0), value)
        for q in range(3):
            value = jnp.where(quantity == 2 + q, conic[q][v : v + 1], value)
        for b in range(blocks):
            attrs[me, 8 + v * view_rows + 8 * b : 16 + v * view_rows + 8 * b, :] = value[
                :, 128 * b : 128 * b + 128
            ]
    base = mg * (own * n_tile)
    spare = attrs.shape[1] - id_row
    attrs[me, 0:8, :] = jnp.zeros((8, 128), jnp.float32)
    attrs[me, id_row:, :] = jnp.zeros((spare, 128), jnp.float32)
    for b in range(blocks):
        attrs[me, b : b + 1, :] = opacity[
            :, 128 * b : 128 * b + 128
        ]
    for v in range(VIEWS):
        ids = (lists_ref[v] - base).astype(jnp.float32)
        for h in range(size // 128):
            place = id_row + v * (size // 128) + h
            attrs[me, place : place + 1, :] = ids[:, 128 * h : 128 * h + 128]

    pl.semaphore_wait(barrier, n_tile + n_gauss - 2)
    sends = []
    for v in range(VIEWS):
        start = 8 + v * view_rows if v > 0 else 0
        stop = 8 + (v + 1) * view_rows if v < VIEWS - 1 else attrs.shape[1]
        for d in range(1, n_tile):
            copy = pltpu.make_async_remote_copy(
                src_ref=attrs.at[me, start:stop],
                dst_ref=attrs.at[me, start:stop],
                send_sem=send_a.at[v, d],
                recv_sem=recv_a.at[v, d],
                device_id={"tile": lax.rem(me + d, n_tile)},
                device_id_type=MESH,
            )
            copy.start()
            sends.append((v, copy))

    before_j = (iota((size, size), 0) < iota((size, size), 1)).astype(jnp.float32)
    after_j = (iota((size, size), 0) > iota((size, size), 1)).astype(jnp.float32)
    for c in range(2):
        upper[c * size : (c + 1) * size, :] = before_j.astype(jnp.bfloat16)
        lower[c * size : (c + 1) * size, :] = after_j.astype(jnp.bfloat16)
    parts[me, rows + 2 * VIEWS : rows + 8, :] = jnp.zeros((8 - 2 * VIEWS, size), jnp.float32)
    grad_sends = []
    pixel_col = iota((16, size), 0).astype(jnp.float32) + 0.5
    lane = iota((1, size), 1)
    low_of = iota((128, size), 0)
    op_row = iota((8 * n_tile, size), 0)
    op_high = jnp.where(op_row % 8 < blocks, op_row // 8 * blocks + op_row % 8, -1)
    for v in range(VIEWS):
        ids = lists_ref[v] - base
        high, low = ids // 128, ids % 128
        onehot = (low_of == low).astype(jnp.float32).astype(jnp.bfloat16)
        for view, copy in sends:
            if view == v:
                copy.wait()
        tiles = [
            attrs[s, 8 + v * view_rows : 8 + (v + 1) * view_rows, :] for s in range(n_tile)
        ] + [attrs[s, 0:8, :] for s in range(n_tile)]
        pieces = jnp.concatenate(split(jnp.concatenate(tiles, axis=0), 3), axis=1)
        picked = dot(pieces, jnp.concatenate([onehot] * 3, axis=0), ((1,), (0,)))
        splat = jnp.zeros((8, size), jnp.float32)
        for h in range(n_tile * blocks):
            splat = jnp.where(high == h, picked[8 * h : 8 * h + 8], splat)
        opac = jnp.sum(
            jnp.where(op_high == high, picked[8 * n_tile * blocks :], 0.0), axis=0, keepdims=True
        )
        mean_x, mean_y = splat[0:1], splat[1:2]
        con0, con1, con2 = splat[2:3], splat[3:4], splat[4:5]
        tile = tile_ids[v]
        corner_x = (tile % TILES_WIDE * 16).astype(jnp.float32)
        corner_y = (tile // TILES_WIDE * 16).astype(jnp.float32)
        live = lane < counts[v]
        dx = pixel_col + corner_x - mean_x
        part_x = -0.5 * con0 * dx * dx
        opac_live = jnp.where(live, opac, 0.0)
        dys = []
        for r in range(16):
            dy = (corner_y + (r + 0.5)) - mean_y
            dys.append(dy)
            exponent = part_x - 0.5 * con2 * dy * dy - (con1 * dy) * dx
            raw = jnp.where(live, opac_live * jnp.exp(exponent), 0.0)
            cover = jnp.minimum(0.99, raw)
            log_keep = jnp.log(1.0 - cover)
            alpha_ref[16 * r : 16 * r + 16, :] = cover
            raw_ref[16 * r : 16 * r + 16, :] = jnp.where(
                raw < 0.99, raw, jnp.where(raw == 0.99, 0.5 * raw, 0.0)
            )
            for c, piece in enumerate(split(log_keep, 2)):
                log_ref[16 * r : 16 * r + 16, c * size : (c + 1) * size] = piece
        trans = jnp.exp(dot(log_ref[...], upper[...], ((1,), (0,))))
        cover = alpha_ref[...]
        weights = cover * trans
        w_split = split(weights, 2)
        colour = jnp.where(iota((8, size), 0) < 3, jnp.concatenate([splat[5:8], splat[0:5]], axis=0), 0.0)
        c_split = jnp.concatenate([p.astype(jnp.float32) for p in split(colour, 3)], axis=0)
        c_split = jnp.concatenate([c_split, jnp.zeros_like(colour)], axis=0).astype(jnp.bfloat16)
        image = dot(c_split, w_split[0], ((1,), (1,))) + dot(c_split, w_split[1], ((1,), (1,)))
        image = image[0:8] + image[8:16] + image[16:24]
        residuals = []
        square = jnp.zeros((1, 256), jnp.float32)
        for k in range(3):
            image_ref[v, k] = image[k : k + 1]
            residual = image[k : k + 1] - target_ref[v, k]
            square = square + residual * residual
            residuals.append(residual * scale)
        resid = jnp.concatenate(residuals + [jnp.zeros((5, 256), jnp.float32)], axis=0)
        slope = dot(resid, colour, ((0,), (0,)), highest)
        later = dot(
            jnp.concatenate(split(weights * slope, 2), axis=1), lower[...], ((1,), (0,))
        )
        moved = (trans * slope - later / (1.0 - cover)) * raw_ref[...]
        r_split = jnp.concatenate([p.astype(jnp.float32) for p in split(resid, 3)], axis=0)
        r_split = jnp.concatenate([r_split, jnp.zeros_like(resid)], axis=0).astype(jnp.bfloat16)
        d_colour = dot(r_split, w_split[0], ((1,), (0,))) + dot(r_split, w_split[1], ((1,), (0,)))
        d_colour = d_colour[0:8] + d_colour[8:16] + d_colour[16:24]
        sum0 = jnp.zeros((16, size), jnp.float32)
        sum1 = jnp.zeros((16, size), jnp.float32)
        sum2 = jnp.zeros((16, size), jnp.float32)
        for r in range(16):
            chunk = moved[16 * r : 16 * r + 16]
            first = chunk * dys[r]
            sum0 = sum0 + chunk
            sum1 = sum1 + first
            sum2 = sum2 + first * dys[r]
        m_0 = jnp.sum(sum0, axis=0, keepdims=True)
        m_x = jnp.sum(sum0 * dx, axis=0, keepdims=True)
        m_xx = jnp.sum(sum0 * dx * dx, axis=0, keepdims=True)
        m_y = jnp.sum(sum1, axis=0, keepdims=True)
        m_xy = jnp.sum(sum1 * dx, axis=0, keepdims=True)
        m_yy = jnp.sum(sum2, axis=0, keepdims=True)
        parts[me, 8 * v : 8 * v + 8, :] = jnp.concatenate(
            [
                con0 * m_x + con1 * m_y,
                con1 * m_x + con2 * m_y,
                -0.5 * m_xx,
                -m_xy,
                -0.5 * m_yy,
                d_colour[0:3],
            ],
            axis=0,
        )
        parts[me, rows + v : rows + v + 1, :] = m_0
        parts[me, rows + VIEWS + v : rows + VIEWS + v + 1, :] = square
        start, stop = 8 * v, (8 * v + 8 if v < VIEWS - 1 else rows + 8)
        for d in range(1, n_tile):
            copy = pltpu.make_async_remote_copy(
                src_ref=parts.at[me, start:stop],
                dst_ref=parts.at[me, start:stop],
                send_sem=send_g.at[v, d],
                recv_sem=recv_g.at[v, d],
                device_id={"tile": lax.rem(me + d, n_tile)},
                device_id_type=MESH,
            )
            copy.start()
            grad_sends.append(copy)

    for copy in grad_sends:
        copy.wait()
    squares = sum(parts[s, rows : rows + 8, :] for s in range(n_tile))
    totals[mg] = squares
    loss_sends = []
    for d in range(1, n_gauss):
        copy = pltpu.make_async_remote_copy(
            src_ref=totals.at[mg],
            dst_ref=totals.at[mg],
            send_sem=send_l.at[d],
            recv_sem=recv_l.at[d],
            device_id={"gauss": lax.rem(mg + d, n_gauss)},
            device_id_type=MESH,
        )
        copy.start()
        loss_sends.append(copy)

    op_block = iota((8, size), 0)
    d_views = []
    d_opacity = jnp.zeros((8, 128), jnp.float32)
    for v in range(VIEWS):
        total = jnp.zeros((8 * blocks + 8, 128), jnp.float32)
        for s in range(n_tile):
            place = id_row + v * (size // 128)
            ids = jnp.concatenate(
                [attrs[s, place + h : place + h + 1, :] for h in range(size // 128)], axis=1
            ).astype(jnp.int32)
            block, low = ids // 128 - me * blocks, ids % 128
            onehot = (low_of == low).astype(jnp.float32).astype(jnp.bfloat16)
            part = parts[s, 8 * v : 8 * v + 8, :]
            op_part = parts[s, rows + v : rows + v + 1, :]
            spread = jnp.concatenate(
                [jnp.where(block == b, part, 0.0) for b in range(blocks)]
                + [jnp.where((block == op_block) & (op_block < blocks), op_part, 0.0)],
                axis=0,
            )
            rough = spread.astype(jnp.bfloat16).astype(jnp.float32)
            both = jnp.concatenate([rough, spread - rough], axis=0).astype(jnp.bfloat16)
            added = dot(both, onehot, ((1,), (1,)))
            total = total + added[: 8 * blocks + 8] + added[8 * blocks + 8 :]
        d_views.append(
            jnp.concatenate([total[8 * b : 8 * b + 8] for b in range(blocks)], axis=1)
        )
        d_opacity = d_opacity + total[8 * blocks :]

    d_linear = []
    for v in range(VIEWS):
        value = linear_views[v]
        gate = jnp.where(value > 0.0, 1.0, jnp.where(value == 0.0, 0.5, 0.0))
        d_linear.append(jnp.where(quantity >= 5, gate * d_views[v], d_views[v]))
    grad_ref[...] = dot(table, jnp.concatenate(d_linear, axis=0), ((0,), (0,)), highest)
    g0, g1, g2 = [
        jnp.concatenate([d_views[v][2 + q : 3 + q] for v in range(VIEWS)], axis=0) for q in range(3)
    ]
    q0, q1, q2 = conic
    d_a = -(g0 * q0 * q0 + g1 * q0 * q1 + g2 * q1 * q1)
    d_b = -(2.0 * g0 * q0 * q1 + g1 * (q0 * q2 + q1 * q1) + 2.0 * g2 * q1 * q2)
    d_c = -(g0 * q1 * q1 + g1 * q1 * q2 + g2 * q2 * q2)
    d_axes = [
        [2.0 * d_a * axes[0][j] + d_b * axes[1][j] for j in range(3)],
        [2.0 * d_c * axes[1][j] + d_b * axes[0][j] for j in range(3)],
    ]
    d_mat = [
        [
            jnp.sum(
                affine[0][i] * d_axes[0][j] + affine[1][i] * d_axes[1][j], axis=0, keepdims=True
            )
            for j in range(3)
        ]
        for i in range(3)
    ]
    for j in range(3):
        grad_ref[3 + j : 4 + j, :] = stretch[j] * sum(d_mat[i][j] * rot[i][j] for i in range(3))
    d_rot = [[d_mat[i][j] * stretch[j] for j in range(3)] for i in range(3)]
    sym01, sym02, sym12 = (
        d_rot[0][1] + d_rot[1][0],
        d_rot[0][2] + d_rot[2][0],
        d_rot[1][2] + d_rot[2][1],
    )
    skew01, skew02, skew12 = (
        d_rot[1][0] - d_rot[0][1],
        d_rot[0][2] - d_rot[2][0],
        d_rot[2][1] - d_rot[1][2],
    )
    d_quat = [
        2.0 * (z * skew01 + y * skew02 + x * skew12),
        2.0 * (y * sym01 + z * sym02 - 2.0 * x * (d_rot[1][1] + d_rot[2][2]) + w * skew12),
        2.0 * (x * sym01 + z * sym12 - 2.0 * y * (d_rot[0][0] + d_rot[2][2]) + w * skew02),
        2.0 * (x * sym02 + y * sym12 - 2.0 * z * (d_rot[0][0] + d_rot[1][1]) + w * skew01),
    ]
    along = w * d_quat[0] + x * d_quat[1] + y * d_quat[2] + z * d_quat[3]
    for i, part in enumerate((w, x, y, z)):
        grad_ref[6 + i : 7 + i, :] = (d_quat[i] - part * along) / norm
    d_op = jnp.concatenate([d_opacity[b : b + 1] for b in range(blocks)], axis=1)
    grad_ref[10:11, :] = d_op * (1.0 - opacity)

    for copy in loss_sends:
        copy.wait()
    all_squares = sum(totals[g] for g in range(n_gauss))
    factor = 0.5 / (3 * 256 * n_tile * n_gauss)
    for v in range(VIEWS):
        loss_ref[v] = jnp.sum(all_squares[VIEWS + v : VIEWS + v + 1]) * factor


def adam(
    params_ref, one_ref, two_ref, grad_ref, image_ref, loss_ref, new_ref, first_ref, second_ref,
    images_ref, losses_ref,
):
    row = iota(params_ref.shape, 0)
    rates = jnp.full(params_ref.shape, learning_rates[-1], jnp.float32)
    for i in range(len(learning_rates) - 2, -1, -1):
        if learning_rates[i] != learning_rates[i + 1]:
            rates = jnp.where(row <= i, learning_rates[i], rates)
    gradient = grad_ref[...]
    first = 0.9 * one_ref[...] + 0.1 * gradient
    second = 0.999 * two_ref[...] + 0.001 * gradient * gradient
    first_ref[...] = first
    second_ref[...] = second
    new_ref[...] = params_ref[...] - rates * first / (jnp.sqrt(second) + 1e-15)
    images_ref[...] = image_ref[...]
    for v in range(VIEWS):
        losses_ref[v] = loss_ref[v]


def shards(params, moment_one, moment_two, camera, target, tile_ids, splat_lists, counts):
    n_tile, n_gauss = lax.axis_size("tile"), lax.axis_size("gauss")
    own = params.shape[1]
    size = splat_lists.shape[2]
    blocks = own // 128
    rows = 8 * VIEWS
    id_rows = -(-(VIEWS * (size // 128)) // 8) * 8
    vmem = pl.BlockSpec(memory_space=pltpu.VMEM)
    smem = pl.BlockSpec(memory_space=pltpu.SMEM)
    dma = pltpu.SemaphoreType.DMA
    gradient, images, losses = pl.pallas_call(
        functools.partial(kernel, n_tile, n_gauss),
        out_shape=(
            jax.ShapeDtypeStruct(params.shape, jnp.float32),
            jax.ShapeDtypeStruct(target.shape, jnp.float32),
            jax.ShapeDtypeStruct((VIEWS,), jnp.float32),
        ),
        in_specs=[vmem, smem, vmem, smem, vmem, smem],
        out_specs=(vmem, vmem, smem),
        scratch_shapes=[
            pltpu.VMEM((n_tile, blocks * rows + 8 + id_rows, 128), jnp.float32),
            pltpu.VMEM((n_tile, rows + 8, size), jnp.float32),
            pltpu.VMEM((n_gauss, 8, size), jnp.float32),
            pltpu.VMEM((2 * size, size), jnp.bfloat16),
            pltpu.VMEM((2 * size, size), jnp.bfloat16),
            pltpu.VMEM((256, size), jnp.float32),
            pltpu.VMEM((256, size), jnp.float32),
            pltpu.VMEM((256, 2 * size), jnp.bfloat16),
            dma((VIEWS, n_tile)),
            dma((VIEWS, n_tile)),
            dma((VIEWS, n_tile)),
            dma((VIEWS, n_tile)),
            dma((n_gauss,)),
            dma((n_gauss,)),
        ],
        compiler_params=pltpu.CompilerParams(collective_id=0, has_side_effects=True),
    )(
        params,
        camera,
        target,
        tile_ids.reshape(VIEWS),
        splat_lists,
        counts.reshape(VIEWS),
    )
    like = jax.ShapeDtypeStruct(params.shape, jnp.float32)
    return pl.pallas_call(
        adam,
        out_shape=(like, like, like, jax.ShapeDtypeStruct(target.shape, jnp.float32),
                   jax.ShapeDtypeStruct((VIEWS,), jnp.float32)),
        in_specs=[vmem, vmem, vmem, vmem, vmem, smem],
        out_specs=(vmem, vmem, vmem, vmem, smem),
    )(params, moment_one, moment_two, gradient, images, losses)


def solution(mesh):
    return jax.shard_map(
        shards,
        mesh=mesh,
        in_specs=(
            P(None, ("gauss", "tile")),
            P(None, ("gauss", "tile")),
            P(None, ("gauss", "tile")),
            P(),
            P(None, None, ("gauss", "tile"), None),
            P(None, ("gauss", "tile")),
            P(None, ("gauss", "tile"), None),
            P(None, ("gauss", "tile")),
        ),
        out_specs=(
            P(None, ("gauss", "tile")),
            P(None, ("gauss", "tile")),
            P(None, ("gauss", "tile")),
            P(None, None, ("gauss", "tile"), None),
            P(),
        ),
        check_vma=False,
    )
```

```python
import functools

import jax
import jax.numpy as jnp
from jax import lax
from jax.experimental import pallas as pl
from jax.experimental.pallas import tpu as pltpu
from jax.sharding import PartitionSpec as P

MESH = pl.DeviceIdType.MESH
VIEWS = 3
TILES_WIDE = 4


band_zero = 0.28209479177387814
band_one = 0.4886025119029199
band_two = (
    1.0925484305920792,
    -1.0925484305920792,
    0.31539156525252005,
    -1.0925484305920792,
    0.5462742152960396,
)
band_three = (
    -0.5900435899266435,
    2.890611442640554,
    -0.4570457994644658,
    0.3731763325901154,
    -0.4570457994644658,
    1.445305721320277,
    -0.5900435899266435,
)
learning_rates = (
    (0.00016,) * 3 + (0.005,) * 3 + (0.001,) * 4 + (0.05,) + (0.0025,) * 3 + (0.000125,) * 45
)
highest = lax.Precision.HIGHEST


def split(value, parts):
    pieces = []
    rest = value
    for _ in range(parts - 1):
        piece = rest.astype(jnp.bfloat16)
        pieces.append(piece)
        rest = rest - piece.astype(jnp.float32)
    pieces.append(rest.astype(jnp.bfloat16))
    return pieces


def dot(left, right, dims, precision=None):
    return lax.dot_general(
        left, right, (dims, ((), ())), precision=precision, preferred_element_type=jnp.float32
    )


def harmonics(x, y, z):
    xx, yy, zz = x * x, y * y, z * z
    return [
        band_zero + 0.0 * x,
        -band_one * y,
        band_one * z,
        -band_one * x,
        band_two[0] * x * y,
        band_two[1] * y * z,
        band_two[2] * (2.0 * zz - xx - yy),
        band_two[3] * x * z,
        band_two[4] * (xx - yy),
        band_three[0] * y * (3.0 * xx - yy),
        band_three[1] * x * y * z,
        band_three[2] * y * (4.0 * zz - xx - yy),
        band_three[3] * z * (2.0 * zz - 3.0 * xx - 3.0 * yy),
        band_three[4] * x * (4.0 * zz - xx - yy),
        band_three[5] * z * (xx - yy),
        band_three[6] * x * (xx - 3.0 * yy),
    ]


def iota(shape, dim):
    return lax.broadcasted_iota(jnp.int32, shape, dim)


def basis(camera, n_params):
    rows = 8 * VIEWS
    row, lane = iota((rows, n_params), 0), iota((rows, n_params), 1)
    quantity, view = row % 8, row // 8

    def entry(index):
        value = jnp.full((rows, n_params), camera[VIEWS - 1, index], jnp.float32)
        for v in range(VIEWS - 1):
            value = jnp.where(view == v, camera[v, index], value)
        return value

    out = jnp.zeros((rows, n_params), jnp.float32)
    for k in range(2):
        for i in range(3):
            out = jnp.where((quantity == k) & (lane == i), entry(3 * k + i), out)
    term, channel = (lane - 11) // 3, (lane - 11) % 3
    own = (lane >= 11) & (channel == quantity - 5)
    for i, value in enumerate(harmonics(entry(8), entry(9), entry(10))):
        out = jnp.where(own & (term == i), value, out)
    return out


def part_rows(view):
    if view < VIEWS - 1:
        return 8 * view, 8 * (VIEWS - 1) + view
    return 8 * VIEWS, 8 * VIEWS + 8


def kernel(
    n_tile,
    n_gauss,
    params_hbm,
    camera_hbm,
    target_hbm,
    tiles_hbm,
    lists_hbm,
    counts_hbm,
    grad_ref,
    image_ref,
    loss_ref,
    params_ref,
    camera,
    target_ref,
    tile_ids,
    lists_ref,
    counts,
    attrs,
    parts,
    totals,
    sums,
    upper,
    lower,
    alpha_ref,
    raw_ref,
    log_ref,
    send_a,
    recv_a,
    send_g,
    recv_g,
    send_l,
    recv_l,
    send_s,
    recv_s,
    load_sem,
):
    me, mg = lax.axis_index("tile"), lax.axis_index("gauss")
    n_params, own = params_ref.shape
    blocks = own // 128
    size = lists_ref.shape[2]
    rows = 8 * VIEWS
    view_rows = 8 * blocks
    id_row = 8 + VIEWS * view_rows
    scale = 1.0 / (VIEWS * 256)
    near_first = sorted(range(1, n_tile), key=lambda d: (min(d, n_tile - d), d))

    barrier = pltpu.get_barrier_semaphore()
    for d in range(1, n_tile):
        pl.semaphore_signal(
            barrier, inc=1, device_id={"tile": lax.rem(me + d, n_tile)}, device_id_type=MESH
        )
    for d in range(1, n_gauss):
        pl.semaphore_signal(
            barrier, inc=1, device_id={"gauss": lax.rem(mg + d, n_gauss)}, device_id_type=MESH
        )

    loads = []
    for i, (source, target) in enumerate(
        (
            (camera_hbm, camera),
            (params_hbm, params_ref),
            (lists_hbm, lists_ref),
            (counts_hbm, counts),
            (tiles_hbm, tile_ids),
            (target_hbm, target_ref),
        )
    ):
        copy = pltpu.make_async_copy(source, target, load_sem.at[i])
        copy.start()
        loads.append(copy)
    for copy in loads:
        copy.wait()

    table = basis(camera, n_params)
    view_of = iota((VIEWS, own), 0)

    def entry(index):
        value = jnp.full((VIEWS, own), camera[VIEWS - 1, index], jnp.float32)
        for v in range(VIEWS - 1):
            value = jnp.where(view_of == v, camera[v, index], value)
        return value

    affine = [[entry(3 * k + i) for i in range(3)] for k in range(2)]
    params = params_ref[...]
    quat = [params_ref[6 + i : 7 + i, :] for i in range(4)]
    norm = jnp.sqrt(quat[0] * quat[0] + quat[1] * quat[1] + quat[2] * quat[2] + quat[3] * quat[3])
    w, x, y, z = [part / norm for part in quat]
    rot = [
        [1.0 - 2.0 * (y * y + z * z), 2.0 * (x * y - w * z), 2.0 * (x * z + w * y)],
        [2.0 * (x * y + w * z), 1.0 - 2.0 * (x * x + z * z), 2.0 * (y * z - w * x)],
        [2.0 * (x * z - w * y), 2.0 * (y * z + w * x), 1.0 - 2.0 * (x * x + y * y)],
    ]
    stretch = [jnp.exp(params_ref[3 + j : 4 + j, :]) for j in range(3)]
    axes = [
        [sum(affine[k][i] * (rot[i][j] * stretch[j]) for i in range(3)) for j in range(3)]
        for k in range(2)
    ]
    cov_a = sum(axes[0][j] * axes[0][j] for j in range(3)) + 0.3
    cov_b = sum(axes[0][j] * axes[1][j] for j in range(3))
    cov_c = sum(axes[1][j] * axes[1][j] for j in range(3)) + 0.3
    determinant = cov_a * cov_c - cov_b * cov_b
    conic = [cov_c / determinant, -cov_b / determinant, cov_a / determinant]
    opacity = jax.nn.sigmoid(params_ref[10:11, :])

    linear = dot(table, params, ((1,), (0,)), highest)
    quantity = iota((8, own), 0)
    linear_views = []
    for v in range(VIEWS):
        shift = jnp.where(
            quantity == 0, camera[v, 6], jnp.where(quantity == 1, camera[v, 7], 0.5)
        )
        value = linear[8 * v : 8 * v + 8] + shift
        linear_views.append(value)
        value = jnp.where(quantity >= 5, jnp.maximum(value, 0.0), value)
        for q in range(3):
            value = jnp.where(quantity == 2 + q, conic[q][v : v + 1], value)
        for b in range(blocks):
            attrs[me, 8 + v * view_rows + 8 * b : 16 + v * view_rows + 8 * b, :] = value[
                :, 128 * b : 128 * b + 128
            ]
    base = mg * (own * n_tile)
    spare = attrs.shape[1] - id_row
    attrs[me, 0:8, :] = jnp.zeros((8, 128), jnp.float32)
    attrs[me, id_row:, :] = jnp.zeros((spare, 128), jnp.float32)
    for b in range(blocks):
        attrs[me, b : b + 1, :] = opacity[
            :, 128 * b : 128 * b + 128
        ]
    for v in range(VIEWS):
        ids = (lists_ref[v] - base).astype(jnp.float32)
        for h in range(size // 128):
            place = id_row + v * (size // 128) + h
            attrs[me, place : place + 1, :] = ids[:, 128 * h : 128 * h + 128]

    pl.semaphore_wait(barrier, n_tile + n_gauss - 2)
    sends = []
    for v in range(VIEWS):
        start = 8 + v * view_rows if v > 0 else 0
        stop = 8 + (v + 1) * view_rows if v < VIEWS - 1 else attrs.shape[1]
        for d in near_first:
            copy = pltpu.make_async_remote_copy(
                src_ref=attrs.at[me, start:stop],
                dst_ref=attrs.at[me, start:stop],
                send_sem=send_a.at[v, d],
                recv_sem=recv_a.at[v, d],
                device_id={"tile": lax.rem(me + d, n_tile)},
                device_id_type=MESH,
            )
            copy.start()
            sends.append((v, copy))

    before_j = (iota((size, size), 0) < iota((size, size), 1)).astype(jnp.float32)
    after_j = (iota((size, size), 0) > iota((size, size), 1)).astype(jnp.float32)
    for c in range(2):
        upper[c * size : (c + 1) * size, :] = before_j.astype(jnp.bfloat16)
        lower[c * size : (c + 1) * size, :] = after_j.astype(jnp.bfloat16)
    parts[me, 8 * VIEWS - 8 : 8 * VIEWS, :] = jnp.zeros((8, size), jnp.float32)
    grad_sends, loss_sends, squares = [], [], []
    pixel_col = iota((16, size), 0).astype(jnp.float32) + 0.5
    lane = iota((1, size), 1)
    low_of = iota((128, size), 0)
    op_row = iota((8 * n_tile, size), 0)
    op_high = jnp.where(op_row % 8 < blocks, op_row // 8 * blocks + op_row % 8, -1)
    for v in range(VIEWS):
        ids = lists_ref[v] - base
        high, low = ids // 128, ids % 128
        onehot = (low_of == low).astype(jnp.float32).astype(jnp.bfloat16)
        for view, copy in sends:
            if view == v:
                copy.wait()
        tiles = [
            attrs[s, 8 + v * view_rows : 8 + (v + 1) * view_rows, :] for s in range(n_tile)
        ] + [attrs[s, 0:8, :] for s in range(n_tile)]
        pieces = jnp.concatenate(split(jnp.concatenate(tiles, axis=0), 3), axis=1)
        picked = dot(pieces, jnp.concatenate([onehot] * 3, axis=0), ((1,), (0,)))
        splat = jnp.zeros((8, size), jnp.float32)
        for h in range(n_tile * blocks):
            splat = jnp.where(high == h, picked[8 * h : 8 * h + 8], splat)
        opac = jnp.sum(
            jnp.where(op_high == high, picked[8 * n_tile * blocks :], 0.0), axis=0, keepdims=True
        )
        mean_x, mean_y = splat[0:1], splat[1:2]
        con0, con1, con2 = splat[2:3], splat[3:4], splat[4:5]
        tile = tile_ids[v]
        corner_x = (tile % TILES_WIDE * 16).astype(jnp.float32)
        corner_y = (tile // TILES_WIDE * 16).astype(jnp.float32)
        live = lane < counts[v]
        dx = pixel_col + corner_x - mean_x
        part_x = -0.5 * con0 * dx * dx
        opac_live = jnp.where(live, opac, 0.0)
        dys = []
        for r in range(16):
            dy = (corner_y + (r + 0.5)) - mean_y
            dys.append(dy)
            exponent = part_x - 0.5 * con2 * dy * dy - (con1 * dy) * dx
            raw = jnp.where(live, opac_live * jnp.exp(exponent), 0.0)
            cover = jnp.minimum(0.99, raw)
            log_keep = jnp.log(1.0 - cover)
            alpha_ref[16 * r : 16 * r + 16, :] = cover
            raw_ref[16 * r : 16 * r + 16, :] = jnp.where(
                raw < 0.99, raw, jnp.where(raw == 0.99, 0.5 * raw, 0.0)
            )
            for c, piece in enumerate(split(log_keep, 2)):
                log_ref[16 * r : 16 * r + 16, c * size : (c + 1) * size] = piece
        trans = jnp.exp(dot(log_ref[...], upper[...], ((1,), (0,))))
        cover = alpha_ref[...]
        weights = cover * trans
        w_split = split(weights, 2)
        colour = jnp.where(iota((8, size), 0) < 3, jnp.concatenate([splat[5:8], splat[0:5]], axis=0), 0.0)
        c_split = jnp.concatenate([p.astype(jnp.float32) for p in split(colour, 3)], axis=0)
        c_split = jnp.concatenate([c_split, jnp.zeros_like(colour)], axis=0).astype(jnp.bfloat16)
        image = dot(c_split, w_split[0], ((1,), (1,))) + dot(c_split, w_split[1], ((1,), (1,)))
        image = image[0:8] + image[8:16] + image[16:24]
        residuals = []
        square = jnp.zeros((1, 256), jnp.float32)
        for k in range(3):
            image_ref[v, k] = image[k : k + 1]
            residual = image[k : k + 1] - target_ref[v, k]
            square = square + residual * residual
            residuals.append(residual * scale)
        squares.append(square[:, 0:128] + square[:, 128:256])
        if v == VIEWS - 1:
            totals[mg] = jnp.concatenate(
                squares + [jnp.zeros((8 - VIEWS, 128), jnp.float32)], axis=0
            )
            for d in range(1, n_gauss):
                copy = pltpu.make_async_remote_copy(
                    src_ref=totals.at[mg],
                    dst_ref=totals.at[mg],
                    send_sem=send_l.at[d],
                    recv_sem=recv_l.at[d],
                    device_id={"gauss": lax.rem(mg + d, n_gauss)},
                    device_id_type=MESH,
                )
                copy.start()
                loss_sends.append(copy)
        resid = jnp.concatenate(residuals + [jnp.zeros((5, 256), jnp.float32)], axis=0)
        slope = dot(resid, colour, ((0,), (0,)), highest)
        later = dot(
            jnp.concatenate(split(weights * slope, 2), axis=1), lower[...], ((1,), (0,))
        )
        moved = (trans * slope - later / (1.0 - cover)) * raw_ref[...]
        r_split = jnp.concatenate([p.astype(jnp.float32) for p in split(resid, 3)], axis=0)
        r_split = jnp.concatenate([r_split, jnp.zeros_like(resid)], axis=0).astype(jnp.bfloat16)
        d_colour = dot(r_split, w_split[0], ((1,), (0,))) + dot(r_split, w_split[1], ((1,), (0,)))
        d_colour = d_colour[0:8] + d_colour[8:16] + d_colour[16:24]
        sum0 = jnp.zeros((16, size), jnp.float32)
        sum1 = jnp.zeros((16, size), jnp.float32)
        sum2 = jnp.zeros((16, size), jnp.float32)
        for r in range(16):
            chunk = moved[16 * r : 16 * r + 16]
            first = chunk * dys[r]
            sum0 = sum0 + chunk
            sum1 = sum1 + first
            sum2 = sum2 + first * dys[r]
        m_0 = jnp.sum(sum0, axis=0, keepdims=True)
        m_x = jnp.sum(sum0 * dx, axis=0, keepdims=True)
        m_xx = jnp.sum(sum0 * dx * dx, axis=0, keepdims=True)
        m_y = jnp.sum(sum1, axis=0, keepdims=True)
        m_xy = jnp.sum(sum1 * dx, axis=0, keepdims=True)
        m_yy = jnp.sum(sum2, axis=0, keepdims=True)
        first_row, op_place = part_rows(v)
        parts[me, first_row : first_row + 8, :] = jnp.concatenate(
            [
                con0 * m_x + con1 * m_y,
                con1 * m_x + con2 * m_y,
                -0.5 * m_xx,
                -m_xy,
                -0.5 * m_yy,
                d_colour[0:3],
            ],
            axis=0,
        )
        parts[me, op_place : op_place + 1, :] = m_0
        start = first_row
        stop = first_row + (8 if v < VIEWS - 2 else 16 if v == VIEWS - 2 else 9)
        for d in near_first:
            copy = pltpu.make_async_remote_copy(
                src_ref=parts.at[me, start:stop],
                dst_ref=parts.at[me, start:stop],
                send_sem=send_g.at[v, d],
                recv_sem=recv_g.at[v, d],
                device_id={"tile": lax.rem(me + d, n_tile)},
                device_id_type=MESH,
            )
            copy.start()
            grad_sends.append((v, copy))

    op_block = iota((8, size), 0)
    d_views = []
    d_opacity = jnp.zeros((8, 128), jnp.float32)
    for v in range(VIEWS):
        if v == VIEWS - 1:
            for copy in loss_sends:
                copy.wait()
            loss_sends = []
            sums[me] = sum(totals[g] for g in range(n_gauss))
            for d in range(1, n_tile):
                copy = pltpu.make_async_remote_copy(
                    src_ref=sums.at[me],
                    dst_ref=sums.at[me],
                    send_sem=send_s.at[d],
                    recv_sem=recv_s.at[d],
                    device_id={"tile": lax.rem(me + d, n_tile)},
                    device_id_type=MESH,
                )
                copy.start()
                loss_sends.append(copy)
        ready = max(v, VIEWS - 2)
        for view, copy in grad_sends:
            if view <= ready:
                copy.wait()
        grad_sends = [pair for pair in grad_sends if pair[0] > ready]
        first_row, op_place = part_rows(v)
        total = jnp.zeros((8 * blocks + 8, 128), jnp.float32)
        for s in range(n_tile):
            place = id_row + v * (size // 128)
            ids = jnp.concatenate(
                [attrs[s, place + h : place + h + 1, :] for h in range(size // 128)], axis=1
            ).astype(jnp.int32)
            block, low = ids // 128 - me * blocks, ids % 128
            onehot = (low_of == low).astype(jnp.float32).astype(jnp.bfloat16)
            part = parts[s, first_row : first_row + 8, :]
            op_part = parts[s, op_place : op_place + 1, :]
            spread = jnp.concatenate(
                [jnp.where(block == b, part, 0.0) for b in range(blocks)]
                + [jnp.where((block == op_block) & (op_block < blocks), op_part, 0.0)],
                axis=0,
            )
            rough = spread.astype(jnp.bfloat16).astype(jnp.float32)
            both = jnp.concatenate([rough, spread - rough], axis=0).astype(jnp.bfloat16)
            added = dot(both, onehot, ((1,), (1,)))
            total = total + added[: 8 * blocks + 8] + added[8 * blocks + 8 :]
        d_views.append(
            jnp.concatenate([total[8 * b : 8 * b + 8] for b in range(blocks)], axis=1)
        )
        d_opacity = d_opacity + total[8 * blocks :]

    d_linear = []
    for v in range(VIEWS):
        value = linear_views[v]
        gate = jnp.where(value > 0.0, 1.0, jnp.where(value == 0.0, 0.5, 0.0))
        d_linear.append(jnp.where(quantity >= 5, gate * d_views[v], d_views[v]))
    grad_ref[...] = dot(table, jnp.concatenate(d_linear, axis=0), ((0,), (0,)), highest)
    g0, g1, g2 = [
        jnp.concatenate([d_views[v][2 + q : 3 + q] for v in range(VIEWS)], axis=0) for q in range(3)
    ]
    q0, q1, q2 = conic
    d_a = -(g0 * q0 * q0 + g1 * q0 * q1 + g2 * q1 * q1)
    d_b = -(2.0 * g0 * q0 * q1 + g1 * (q0 * q2 + q1 * q1) + 2.0 * g2 * q1 * q2)
    d_c = -(g0 * q1 * q1 + g1 * q1 * q2 + g2 * q2 * q2)
    d_axes = [
        [2.0 * d_a * axes[0][j] + d_b * axes[1][j] for j in range(3)],
        [2.0 * d_c * axes[1][j] + d_b * axes[0][j] for j in range(3)],
    ]
    d_mat = [
        [
            jnp.sum(
                affine[0][i] * d_axes[0][j] + affine[1][i] * d_axes[1][j], axis=0, keepdims=True
            )
            for j in range(3)
        ]
        for i in range(3)
    ]
    for j in range(3):
        grad_ref[3 + j : 4 + j, :] = stretch[j] * sum(d_mat[i][j] * rot[i][j] for i in range(3))
    d_rot = [[d_mat[i][j] * stretch[j] for j in range(3)] for i in range(3)]
    sym01, sym02, sym12 = (
        d_rot[0][1] + d_rot[1][0],
        d_rot[0][2] + d_rot[2][0],
        d_rot[1][2] + d_rot[2][1],
    )
    skew01, skew02, skew12 = (
        d_rot[1][0] - d_rot[0][1],
        d_rot[0][2] - d_rot[2][0],
        d_rot[2][1] - d_rot[1][2],
    )
    d_quat = [
        2.0 * (z * skew01 + y * skew02 + x * skew12),
        2.0 * (y * sym01 + z * sym02 - 2.0 * x * (d_rot[1][1] + d_rot[2][2]) + w * skew12),
        2.0 * (x * sym01 + z * sym12 - 2.0 * y * (d_rot[0][0] + d_rot[2][2]) + w * skew02),
        2.0 * (x * sym02 + y * sym12 - 2.0 * z * (d_rot[0][0] + d_rot[1][1]) + w * skew01),
    ]
    along = w * d_quat[0] + x * d_quat[1] + y * d_quat[2] + z * d_quat[3]
    for i, part in enumerate((w, x, y, z)):
        grad_ref[6 + i : 7 + i, :] = (d_quat[i] - part * along) / norm
    d_op = jnp.concatenate([d_opacity[b : b + 1] for b in range(blocks)], axis=1)
    grad_ref[10:11, :] = d_op * (1.0 - opacity)

    for copy in loss_sends:
        copy.wait()
    all_squares = sum(sums[s] for s in range(n_tile))
    factor = 0.5 / (3 * 256 * n_tile * n_gauss)
    for v in range(VIEWS):
        loss_ref[v] = jnp.sum(all_squares[v : v + 1]) * factor


def adam(
    params_ref, one_ref, two_ref, grad_ref, image_ref, loss_ref, new_ref, first_ref, second_ref,
    images_ref, losses_ref,
):
    row = iota(params_ref.shape, 0)
    rates = jnp.full(params_ref.shape, learning_rates[-1], jnp.float32)
    for i in range(len(learning_rates) - 2, -1, -1):
        if learning_rates[i] != learning_rates[i + 1]:
            rates = jnp.where(row <= i, learning_rates[i], rates)
    gradient = grad_ref[...]
    first = 0.9 * one_ref[...] + 0.1 * gradient
    second = 0.999 * two_ref[...] + 0.001 * gradient * gradient
    first_ref[...] = first
    second_ref[...] = second
    new_ref[...] = params_ref[...] - rates * first / (jnp.sqrt(second) + 1e-15)
    images_ref[...] = image_ref[...]
    for v in range(VIEWS):
        losses_ref[v] = loss_ref[v]


def shards(params, moment_one, moment_two, camera, target, tile_ids, splat_lists, counts):
    n_tile, n_gauss = lax.axis_size("tile"), lax.axis_size("gauss")
    own = params.shape[1]
    size = splat_lists.shape[2]
    blocks = own // 128
    rows = 8 * VIEWS
    id_rows = -(-(VIEWS * (size // 128)) // 8) * 8
    vmem = pl.BlockSpec(memory_space=pltpu.VMEM)
    smem = pl.BlockSpec(memory_space=pltpu.SMEM)
    dma = pltpu.SemaphoreType.DMA
    gradient, images, losses = pl.pallas_call(
        functools.partial(kernel, n_tile, n_gauss),
        out_shape=(
            jax.ShapeDtypeStruct(params.shape, jnp.float32),
            jax.ShapeDtypeStruct(target.shape, jnp.float32),
            jax.ShapeDtypeStruct((VIEWS,), jnp.float32),
        ),
        in_specs=[pl.BlockSpec(memory_space=pltpu.HBM)] * 6,
        out_specs=(vmem, vmem, smem),
        scratch_shapes=[
            pltpu.VMEM(params.shape, jnp.float32),
            pltpu.SMEM(camera.shape, jnp.float32),
            pltpu.VMEM(target.shape, jnp.float32),
            pltpu.SMEM((VIEWS,), jnp.int32),
            pltpu.VMEM(splat_lists.shape, jnp.int32),
            pltpu.SMEM((VIEWS,), jnp.int32),
            pltpu.VMEM((n_tile, blocks * rows + 8 + id_rows, 128), jnp.float32),
            pltpu.VMEM((n_tile, rows + 9, size), jnp.float32),
            pltpu.VMEM((n_gauss, 8, 128), jnp.float32),
            pltpu.VMEM((n_tile, 8, 128), jnp.float32),
            pltpu.VMEM((2 * size, size), jnp.bfloat16),
            pltpu.VMEM((2 * size, size), jnp.bfloat16),
            pltpu.VMEM((256, size), jnp.float32),
            pltpu.VMEM((256, size), jnp.float32),
            pltpu.VMEM((256, 2 * size), jnp.bfloat16),
            dma((VIEWS, n_tile)),
            dma((VIEWS, n_tile)),
            dma((VIEWS, n_tile)),
            dma((VIEWS, n_tile)),
            dma((n_gauss,)),
            dma((n_gauss,)),
            dma((n_tile,)),
            dma((n_tile,)),
            dma((6,)),
        ],
        compiler_params=pltpu.CompilerParams(collective_id=0, has_side_effects=True),
    )(
        params,
        camera,
        target,
        tile_ids.reshape(VIEWS),
        splat_lists,
        counts.reshape(VIEWS),
    )
    like = jax.ShapeDtypeStruct(params.shape, jnp.float32)
    return pl.pallas_call(
        adam,
        out_shape=(like, like, like, jax.ShapeDtypeStruct(target.shape, jnp.float32),
                   jax.ShapeDtypeStruct((VIEWS,), jnp.float32)),
        in_specs=[vmem, vmem, vmem, vmem, vmem, smem],
        out_specs=(vmem, vmem, vmem, vmem, smem),
    )(params, moment_one, moment_two, gradient, images, losses)


def solution(mesh):
    return jax.shard_map(
        shards,
        mesh=mesh,
        in_specs=(
            P(None, ("gauss", "tile")),
            P(None, ("gauss", "tile")),
            P(None, ("gauss", "tile")),
            P(),
            P(None, None, ("gauss", "tile"), None),
            P(None, ("gauss", "tile")),
            P(None, ("gauss", "tile"), None),
            P(None, ("gauss", "tile")),
        ),
        out_specs=(
            P(None, ("gauss", "tile")),
            P(None, ("gauss", "tile")),
            P(None, ("gauss", "tile")),
            P(None, None, ("gauss", "tile"), None),
            P(),
        ),
        check_vma=False,
    )
```
